32 devices in a mesh: dp: 16 (over z, y, x), expert: 2 (over core).
Axes of the slice: x: 2, y: 2, z: 4, core: 2. Of those that a mesh axis runs over, the one named last changes fastest.
Arguments:
- hidden: bfloat16 [2, 16384, 1024], P('expert', 'dp'), may hold values from -6 to 6
- cotangent: bfloat16 [2, 16384, 3584], P('expert', 'dp'), may hold values from -6 to 6
- counts: int32 [2, 16], P('expert', 'dp'), may hold values from 1 to 1024, as said below
- placement: int32 [2, 4], replicated, may hold values from 0 to 1, as said below
- weight: bfloat16 [2, 1024, 3584], P('expert', 'dp'), may hold values from -4 to 4
- moment: float32 [2, 1024, 3584], P('expert', 'dp'), may hold values from -2 to 2
- second: float32 [2, 1024, 3584], P('expert', 'dp'), may hold values from 0.005 to 1
- serving: bfloat16 [2, 4, 1024, 3584], P('expert', None, 'dp'), may hold values from -4 to 4
Outputs:
- d_hidden: bfloat16 [2, 16384, 1024], P('expert', 'dp')
- new_weight: bfloat16 [2, 1024, 3584], P('expert', 'dp')
- new_moment: float32 [2, 1024, 3584], P('expert', 'dp')
- new_second: float32 [2, 1024, 3584], P('expert', 'dp')
- served: bfloat16 [2, 4, 1024, 3584], P('expert', None, 'dp')
The draws below stay inside these ranges and needn't reach their ends.
Inputs may be any that keep to these rules, and one draw needn't show every extreme that they name: `counts`: every count is reached by some expert and data shard in every draw at its upper end, 1024. `placement`: some two groups hold different experts as their first replica.
All inputs are finite; a program needn't handle non-finite values.
Results may differ from the reference program's by a relative error of at most 0.0012.
Values may be sent and summed in bfloat16 or wider, within the bound.
No kernel may reach another device: no remote copies, remote signals or barrier semaphores. Data moves between devices by JAX's collectives and lax.ppermute only.
A program may use at most 128 MiB of HBM per device.

```python
import math
import jax
import jax.numpy as jnp
from jax import lax

D = 3584
FF = 1024
TOK = 1024
REPL = 4
EXPERTS = 2
N_DP = 16


def draw_counts(key, part):
    key_level, key_base, key_row, key_col = jax.random.split(jax.random.fold_in(key, 17), 4)
    level = jax.random.randint(key_level, (EXPERTS, 1), 1, 5)
    base = jax.random.randint(key_base, (EXPERTS, N_DP), TOK // 8, TOK // 4 + 1)
    loads = jnp.minimum(base * level, TOK)
    row_pick = jax.random.randint(key_row, (), 0, EXPERTS)
    col_pick = jax.random.randint(key_col, (), 0, N_DP)
    loads = loads.at[row_pick, col_pick].set(TOK)
    return loads.astype(jnp.int32)


def draw_placement(key, part):
    key_base, key_pick, key_shift = jax.random.split(jax.random.fold_in(key, 29), 3)
    groups = jax.random.randint(key_base, (EXPERTS, REPL), 0, EXPERTS)
    chosen = jax.random.randint(key_pick, (), 0, EXPERTS)
    neighbour = groups[(chosen + 1) % EXPERTS, 0]
    offset = jax.random.randint(key_shift, (), 1, EXPERTS)
    groups = groups.at[chosen, 0].set((neighbour + offset) % EXPERTS)
    return groups.astype(jnp.int32)


def levels(own_key, extent, cuts, low, top_value):
    level, own = 1.0, jax.random.fold_in(own_key, 6)
    for axis_at, shards_of in cuts:
        heights = jnp.exp(jax.random.uniform(jax.random.fold_in(own, axis_at), (shards_of,), jnp.float32, low / len(cuts), top_value / len(cuts)))
        level = level * jnp.repeat(heights, extent[axis_at] // shards_of).reshape([-1 if axis == axis_at else 1 for axis in range(len(extent))])
    return level


def bell_draw(rng, extent, deviation, most, shards=(), held_as=jnp.bfloat16):
    values = deviation * jax.random.normal(rng, extent, jnp.float32)
    if shards:
        values = values * levels(rng, extent, shards, -0.22, 0.18)
    return jnp.clip(values, -most, most).astype(held_as)


def setup_inputs(seed: int = 0) -> dict:
    seeds = jax.random.split(jax.random.key(seed), 9)
    hidden = bell_draw(seeds[0], (EXPERTS, N_DP * TOK, FF), 1.0, 6.0, ((0, 2), (1, 16)))
    cotangent = bell_draw(seeds[1], (EXPERTS, N_DP * TOK, D), 1.0, 6.0, ((0, 2), (1, 16)))
    counts = draw_counts(jax.random.fold_in(seeds[8], 71), 0)
    placement = draw_placement(jax.random.fold_in(seeds[8], 71), 0)
    weight = bell_draw(seeds[4], (EXPERTS, FF, D), 1.0, 4.0, ((0, 2), (1, 16)))
    moment = bell_draw(seeds[5], (EXPERTS, FF, D), 0.3, 2.0, ((0, 2), (1, 16)), jnp.float32)
    second = jnp.clip(jnp.exp(math.log(1.0) - 5.2983174 * jax.random.uniform(seeds[6], (EXPERTS, FF, D), jnp.float32) ** levels(seeds[6], (EXPERTS, FF, D), ((0, 2), (1, 16)), -0.2, 0.2)), 0.005, 1.0)
    serving = bell_draw(seeds[7], (EXPERTS, REPL, FF, D), 1.0, 4.0, ((0, 2), (2, 16)))
    return dict(hidden=hidden, cotangent=cotangent, counts=counts, placement=placement, weight=weight, moment=moment, second=second, serving=serving)


beta_one = 0.9
beta_two = 0.95
bias_one = 1.0 - 0.9 ** 20
bias_two = 1.0 - 0.95 ** 20
learn_rate = 0.05
decay_rate = 0.1
epsilon = 1e-08

def reference(hidden, cotangent, counts, placement, weight, moment, second, serving):
    scale = D ** (-0.5)
    slots = jnp.arange(N_DP * TOK, dtype=jnp.int32)
    position = slots % TOK
    shard = slots // TOK

    def one_expert(operands):
        acts, grads_out, limit, matrix, first, squares = operands
        live = position < limit[shard]
        masked = jnp.where(live[:, None], grads_out, jnp.zeros_like(grads_out))
        d_hid = (scale * jnp.dot(masked, matrix.T, preferred_element_type=jnp.float32)).astype(jnp.bfloat16)
        grad = scale * jnp.dot(acts.T, masked, preferred_element_type=jnp.float32)
        first_new = beta_one * first + (1.0 - beta_one) * grad
        squares_new = beta_two * squares + (1.0 - beta_two) * grad * grad
        step = first_new / bias_one / (jnp.sqrt(squares_new / bias_two) + epsilon)
        current = matrix.astype(jnp.float32)
        updated = current - learn_rate * (step + decay_rate * current)
        delta = (updated - current).astype(jnp.bfloat16)
        return (d_hid, updated.astype(jnp.bfloat16), first_new, squares_new, delta)
    d_hidden, new_weight, new_moment, new_second, delta = lax.map(one_expert, (hidden, cotangent, counts, weight, moment, second))
    picked = jnp.take(delta, placement.astype(jnp.int32), axis=0)
    served = (serving.astype(jnp.float32) + picked.astype(jnp.float32)).astype(jnp.bfloat16)
    return (d_hidden, new_weight, new_moment, new_second, served)
```

```python
import math

import jax
import jax.numpy as jnp
from jax import lax
from jax.sharding import PartitionSpec as P


beta_one = 0.9
beta_two = 0.95
bias_one = 1.0 - 0.9**20
bias_two = 1.0 - 0.95**20
learn_rate = 0.05
decay_rate = 0.1
epsilon = 1e-08
largest_input = 6.0
half_range = 60000.0


def pairs_across(count, bit):
    return [(i, i ^ bit) for i in range(count)]


def pairs_along(count, step, first, last):
    return [(i, i + step * 4) for i in range(count) if first <= i // 4 < last]


def pick(stacked, at):
    return lax.dynamic_index_in_dim(stacked, at, 0, keepdims=False)


def gather_half(own, near_bit, far_bit, outer, count):
    depth = count // 4
    other = lax.ppermute(own, "dp", pairs_across(count, near_bit))
    base = jnp.stack([own, other])
    below, above = {}, {}
    up = down = base
    for t in range(1, depth):
        up = below[t] = lax.ppermute(up, "dp", pairs_along(count, 1, t - 1, depth - 1))
        down = above[t] = lax.ppermute(down, "dp", pairs_along(count, -1, 1, depth - t + 1))
    near = [base]
    for k in range(1, depth):
        near.append(jnp.where(outer + k < depth, above[k], below[depth - k]))
    far = [lax.ppermute(piece, "dp", pairs_across(count, far_bit)) for piece in near]
    return near, far


def reduce_half(send, keep, first_bit, last_bit, last, outer, count):
    depth = count // 4
    order = []
    for t in range(1, depth // 2 + 1):
        for k in (depth - t, t):
            if k not in order:
                order.append(k)
    order.append(0)
    total = {}
    for k in order:
        at = lax.rem(outer + k, depth)
        came = lax.ppermute(pick(send, at), "dp", pairs_across(count, first_bit))
        total[k] = pick(keep, at) + came.astype(jnp.float32)
    up = down = None
    for t in range(1, depth):
        rise, fall = total[depth - t], total[t]
        if up is not None:
            rise = rise + up.astype(jnp.float32)
            fall = fall + down.astype(jnp.float32)
        up = lax.ppermute(rise.astype(jnp.float16), "dp", pairs_along(count, 1, 0, t))
        down = lax.ppermute(fall.astype(jnp.float16), "dp", pairs_along(count, -1, depth - t, depth))
    whole = total[0]
    if up is not None:
        whole = whole + up.astype(jnp.float32) + down.astype(jnp.float32)
    out = pick(whole, 1 - last).astype(jnp.float16)
    came = lax.ppermute(out, "dp", pairs_across(count, last_bit))
    return pick(whole, last) + came.astype(jnp.float32)


def on_device(hidden, cotangent, counts, placement, weight, moment, second, serving):
    acts = hidden[0]
    grads_out = cotangent[0]
    matrix = weight[0]
    tokens, rows = acts.shape
    owned, width = matrix.shape
    scale = width ** (-0.5)
    count = lax.axis_size("dp")
    depth = count // 4
    place = lax.axis_index("dp")
    outer, upper, lower = place // 4, lax.rem(place // 2, 2), lax.rem(place, 2)
    cut = width // 2
    live = jnp.arange(tokens, dtype=jnp.int32) < counts[0, 0]

    bound = count * tokens * largest_input**2 * scale
    lift = 2.0 ** math.floor(math.log2(half_range / bound))

    near_a, far_a = gather_half(matrix[:, :cut], 2, 1, outer, count)
    near_b, far_b = gather_half(matrix[:, cut:], 1, 2, outer, count)

    turned = jnp.where(live[:, None], acts, jnp.zeros_like(acts)).T
    turned = lax.optimization_barrier(turned)
    turned = turned.reshape(depth, 2, 2, owned, tokens)

    def term(axis, at, columns):
        picked = lax.dynamic_index_in_dim(turned, at, axis, keepdims=False)
        picked = picked.reshape(-1, tokens)
        product = jnp.dot(picked, columns, preferred_element_type=jnp.float32)
        return ((scale * lift) * product).reshape(depth, 2, owned, cut)

    columns_a, columns_b = grads_out[:, :cut], grads_out[:, cut:]
    send_a = term(2, 1 - lower, columns_a).astype(jnp.float16)
    send_b = term(1, 1 - upper, columns_b).astype(jnp.float16)
    keep_a = term(2, lower, columns_a)
    keep_b = term(1, upper, columns_b)
    grad_a = reduce_half(send_a, keep_a, 1, 2, upper, outer, count)
    grad_b = reduce_half(send_b, keep_b, 2, 1, lower, outer, count)

    groups = lax.axis_size("expert")
    mine = lax.axis_index("expert")
    wanted = pick(placement, mine)

    def finish(summed, columns):
        grad = (1.0 / lift) * summed
        first_new = beta_one * moment[0][:, columns] + (1.0 - beta_one) * grad
        squares_new = beta_two * second[0][:, columns] + (1.0 - beta_two) * grad * grad
        step = first_new / bias_one / (jnp.sqrt(squares_new / bias_two) + epsilon)
        current = matrix[:, columns].astype(jnp.float32)
        updated = current - learn_rate * (step + decay_rate * current)
        delta = (updated - current).astype(jnp.bfloat16)
        incoming = jnp.where((wanted == mine)[:, None, None], delta[None], jnp.zeros_like(delta)[None])
        for shift in range(1, groups):
            other = lax.ppermute(delta, "expert", [(e, (e + shift) % groups) for e in range(groups)])
            source = lax.rem(mine + groups - shift, groups)
            incoming = jnp.where((wanted == source)[:, None, None], other[None], incoming)
        served = serving[0][:, :, columns].astype(jnp.float32) + incoming.astype(jnp.float32)
        return updated.astype(jnp.bfloat16), first_new, squares_new, served.astype(jnp.bfloat16)

    done_a = finish(grad_a, slice(0, cut))
    done_b = finish(grad_b, slice(cut, width))
    new_weight, new_moment, new_second, served = (
        jnp.concatenate(two, axis=-1) for two in zip(done_a, done_b)
    )

    def in_order(stacked):
        twice = jnp.concatenate([stacked, stacked])
        return lax.dynamic_slice_in_dim(twice, depth - outer, depth, 0)

    def flip(two, at, axis):
        return jnp.where(at == 0, two, jnp.flip(two, axis))

    whole_a = in_order(jnp.stack([jnp.stack(p, axis=1) for p in zip(near_a, far_a)]))
    whole_a = flip(flip(whole_a, upper, 1), lower, 2)
    whole_b = in_order(jnp.stack([jnp.stack(p, axis=0) for p in zip(near_b, far_b)]))
    whole_b = flip(flip(whole_b, upper, 1), lower, 2)
    full = jnp.concatenate([whole_a, whole_b], axis=-1).reshape(rows, width)
    d_full = scale * jnp.dot(grads_out, full.T, preferred_element_type=jnp.float32)
    d_hid = jnp.where(live[:, None], d_full, 0.0).astype(jnp.bfloat16)
    return d_hid[None], new_weight[None], new_moment[None], new_second[None], served[None]


def solution(mesh):
    placed = (
        P("expert", "dp", None),
        P("expert", "dp", None),
        P("expert", "dp"),
        P(),
        P("expert", "dp", None),
        P("expert", "dp", None),
        P("expert", "dp", None),
        P("expert", None, "dp", None),
    )
    return jax.shard_map(
        on_device,
        mesh=mesh,
        in_specs=placed,
        out_specs=(
            P("expert", "dp", None),
            P("expert", "dp", None),
            P("expert", "dp", None),
            P("expert", "dp", None),
            P("expert", None, "dp", None),
        ),
        check_vma=False,
    )
```

```python
import functools
import math

import jax
import jax.numpy as jnp
from jax import lax
from jax.experimental import pallas as pl
from jax.experimental.pallas import tpu as pltpu
from jax.sharding import PartitionSpec as P


beta_one = 0.9
beta_two = 0.95
bias_one = 1.0 - 0.9**20
bias_two = 1.0 - 0.95**20
learn_rate = 0.05
decay_rate = 0.1
epsilon = 1e-08
largest_input = 6.0
half_range = 60000.0


def pairs_across(count, bit):
    return [(i, i ^ bit) for i in range(count)]


def pairs_around(count, k):
    return [((i + 4 * k) % count, i) for i in range(count)]


def pairs_along(count, step, first, last):
    return [(i, i + step * 4) for i in range(count) if first <= i // 4 < last]


def move(value, pairs, axis="dp"):
    return lax.ppermute(value, axis, pairs)


def after(value, *earlier):
    return lax.optimization_barrier((value,) + earlier)[0] if earlier else value


def pick(stacked, at, axis=0):
    return lax.dynamic_index_in_dim(stacked, at, axis, keepdims=False)


def gather_groups(depth):
    groups = {}
    for k in range(depth):
        groups.setdefault(max(k, depth - k) if k else 0, []).append(k)
    return [groups[t] for t in sorted(groups)]


def reduce_groups(depth):
    offsets = list(range(1, depth)) + [0]
    return [offsets[: depth // 2], offsets[depth // 2 :]]


def rows_kernel(order, place, limit, acts, send, keep, turned):
    depth = 2 * len(order[0])
    half = turned.shape[0] // (8 * depth)
    outer, upper, lower = place[0] // 4, lax.rem(place[0] // 2, 2), lax.rem(place[0], 2)
    values = acts[...]
    at = lax.broadcasted_iota(jnp.int32, values.shape, 0)
    turned[...] = jnp.where(at < limit[0], values, jnp.zeros_like(values)).T
    for out, flipped in ((send, 1), (keep, 0)):
        target = 0
        for g, h in ((0, 0), (0, 1), (1, 0), (1, 1)):
            for k in order[g]:
                z = lax.rem(outer + k, depth)
                for j in range(2):
                    y = upper ^ (1 - j) if h == 0 else upper ^ flipped
                    x = lower ^ flipped if h == 0 else lower ^ (1 - j)
                    source = (((z * 2 + y) * 2 + x) * 2 + h) * half
                    out[pl.ds(target, half)] = turned[pl.ds(pl.multiple_of(source, half), half)]
                    target += half


def rows_by_owner(order, place, limit, acts):
    tokens, rows = acts.shape
    shape = jax.ShapeDtypeStruct((rows // 2, tokens), acts.dtype)
    return pl.pallas_call(
        functools.partial(rows_kernel, order),
        out_shape=(shape, shape),
        grid_spec=pltpu.PrefetchScalarGridSpec(
            num_scalar_prefetch=2,
            grid=(1,),
            in_specs=[pl.BlockSpec((tokens, rows), lambda i, *_: (0, 0))],
            out_specs=[pl.BlockSpec((rows // 2, tokens), lambda i, *_: (0, 0))] * 2,
            scratch_shapes=[pltpu.VMEM((rows, tokens), acts.dtype)],
        ),
        name="rows_by_owner",
    )(place, limit, acts)


def hidden_kernel(groups, place, limit, *refs):
    columns, out, full = refs[-3:]
    upper, lower = lax.rem(place[0] // 2, 2), lax.rem(place[0], 2)
    half = full.shape[1] // 8

    def at(y, x, h):
        return pl.ds(pl.multiple_of(((y * 2 + x) * 2 + h) * half, half), half)

    start = 0
    for size in groups:
        far_a, far_b = refs[size : size + 2]
        for m in range(size):
            n = start + m
            near = refs[m]

            @pl.when((pl.program_id(0) == 0) & (pl.program_id(1) == n))
            def _():
                for j in range(2):
                    y, x = upper ^ j, lower ^ j
                    full[n, at(y, lower, 0)] = near[0, j]
                    full[n, at(y, 1 - lower, 0)] = far_a[m, j]
                    full[n, at(upper, x, 1)] = near[1, j]
                    full[n, at(1 - upper, x, 1)] = far_b[m, j]

        start += size
        refs = refs[size + 2 :]

    product = lax.dot_general(
        columns[...],
        full[pl.program_id(1)],
        (((1,), (1,)), ((), ())),
        preferred_element_type=jnp.float32,
    )
    product = columns.shape[1] ** (-0.5) * product
    first = pl.program_id(0) * product.shape[0]
    token = first + lax.broadcasted_iota(jnp.int32, product.shape, 0)
    out[...] = jnp.where(token < limit[0], product, 0.0).astype(out.dtype)


def hidden_columns(place, limit, groups, columns, so_far, depth):
    tokens, width = columns.shape
    offsets = [k for group, _ in groups for k in group]
    block = 8 * groups[0][1][0].shape[2]
    steps = 2

    def slot(place, k):
        return lax.rem(place[0] // 4 + k, depth)

    def same(array):
        zeros = (0,) * array.ndim
        return pl.BlockSpec(array.shape, lambda t, n, *_: zeros, pipeline_mode=pl.Buffered(1))

    in_specs, args = [], [place, limit]
    for _, arrays in groups:
        in_specs += [same(array) for array in arrays]
        args += arrays
    in_specs.append(pl.BlockSpec((tokens // steps, width), lambda t, n, *_: (t, 0)))
    args.append(columns)
    aliases = {}
    kernel = functools.partial(hidden_kernel, [len(group) for group, _ in groups])
    if so_far is not None:
        in_specs.insert(0, pl.BlockSpec(memory_space=pl.ANY))
        args.insert(2, so_far)
        aliases = {2: 0}
        inner = kernel
        kernel = lambda place, limit, so_far, *refs: inner(place, limit, *refs)

    def target(t, n, place, limit):
        at = slot(place, offsets[0])
        for m, k in enumerate(offsets[1:], 1):
            at = jnp.where(n == m, slot(place, k), at)
        return t, at

    return pl.pallas_call(
        kernel,
        out_shape=jax.ShapeDtypeStruct((tokens, depth * block), jnp.bfloat16),
        grid_spec=pltpu.PrefetchScalarGridSpec(
            num_scalar_prefetch=2,
            grid=(steps, len(offsets)),
            in_specs=in_specs,
            out_specs=pl.BlockSpec((tokens // steps, block), target),
            scratch_shapes=[pltpu.VMEM((len(offsets), block, width), jnp.bfloat16)],
        ),
        input_output_aliases=aliases,
        cost_estimate=pl.CostEstimate(
            flops=2 * tokens * width * block * len(offsets),
            transcendentals=0,
            bytes_accessed=2 * tokens * width,
        ),
        name="hidden_columns",
    )(*args)


def body(hidden, cotangent, counts, placement, weight, moment, second, serving):
    acts = hidden[0]
    grads_out = cotangent[0]
    matrix = weight[0]
    tokens, rows = acts.shape
    owned, width = matrix.shape
    scale = width ** (-0.5)
    count = lax.axis_size("dp")
    depth = count // 4
    index = lax.axis_index("dp")
    outer, upper, lower = index // 4, lax.rem(index // 2, 2), lax.rem(index, 2)
    half = owned // 2
    place = jnp.full((1,), index, jnp.int32)
    limit = counts[0]
    across_x, across_y = pairs_across(count, 1), pairs_across(count, 2)
    by_kernel = half % 16 == 0

    bound = count * tokens * largest_input**2 * scale
    lift = 2.0 ** math.floor(math.log2(half_range / bound))

    own_a, own_b = matrix[:half], matrix[half:]
    other_a = move(own_a, across_y)
    other_b = move(own_b, across_x)
    base = jnp.stack([jnp.stack([own_a, other_a]), jnp.stack([own_b, other_b])])
    below, above = {}, {}
    up = down = base
    for t in range(1, depth):
        up = below[t] = move(up, pairs_along(count, 1, t - 1, depth - 1))
        down = above[t] = move(down, pairs_along(count, -1, 1, depth - t + 1))
    near = {0: base}
    for k in range(1, depth):
        near[k] = jnp.where(outer + k < depth, above[k], below[depth - k])
    gathered = []
    for group in gather_groups(depth):
        far_a = move(jnp.stack([near[k][0] for k in group]), across_x)
        far_b = move(jnp.stack([near[k][1] for k in group]), across_y)
        gathered.append((group, [near[k] for k in group] + [far_a, far_b]))

    order = reduce_groups(depth)
    if by_kernel:
        send_rows, keep_rows = rows_by_owner(order, place, limit, acts)
    else:
        live = jnp.arange(tokens, dtype=jnp.int32) < limit[0]
        turned = jnp.where(live[:, None], acts, jnp.zeros_like(acts)).T
        turned = turned.reshape(depth, 2, 2, 2, half, tokens)
        turned = jnp.stack([pick(turned, lax.rem(outer + k, depth)) for k in sum(order, [])])

        def by_side(flipped):
            part_a = pick(turned[:, :, :, 0], lower ^ flipped, 2)
            part_b = pick(turned[:, :, :, 1], upper ^ flipped, 1)
            part_a = jnp.stack([pick(part_a, 1 - upper, 1), pick(part_a, upper, 1)], axis=1)
            part_b = jnp.stack([pick(part_b, 1 - lower, 1), pick(part_b, lower, 1)], axis=1)
            both = jnp.stack([part_a, part_b]).reshape(2, 2, depth // 2, 2, half, tokens)
            return jnp.swapaxes(both, 0, 1).reshape(-1, tokens)

        send_rows, keep_rows = by_side(1), by_side(0)

    def term(picked, kind):
        product = jnp.dot(picked, grads_out, preferred_element_type=jnp.float32)
        product = ((scale * lift) * product).astype(kind)
        return product.reshape(-1, 2, depth // 2, 2, half, width)

    def wide(value):
        return value.astype(jnp.float32)

    came = []
    for g in range(2):
        some = send_rows[g * rows // 4 : (g + 1) * rows // 4]
        send = term(some, jnp.float16)[0]
        came_a = move(send[0], across_x)
        came_b = move(send[1], across_y)
        came.append((came_a, came_b))
    keep = term(keep_rows, jnp.float32)
    sent, middle = (), []
    for g in range(2):
        came_a, came_b = came[g]
        kept = after(keep, *sent)
        out_a = (kept[g, 0, :, 0] + wide(came_a[:, 0])).astype(jnp.float16)
        out_b = (kept[g, 1, :, 0] + wide(came_b[:, 0])).astype(jnp.float16)
        second_a = move(out_a, across_y)
        second_b = move(out_b, across_x)
        middle.append((second_a, second_b))
        sent = (out_a, out_b)
    parts, total = [], None
    for g in range(2):
        came_a, came_b = came[g]
        second_a, second_b = (after(value, *sent) for value in middle[g])
        leaving = []
        for n, k in enumerate(order[g]):
            sum_a = keep[g, 0, n, 1] + wide(came_a[n, 1]) + wide(second_a[n])
            sum_b = keep[g, 1, n, 1] + wide(came_b[n, 1]) + wide(second_b[n])
            joined = jnp.concatenate([sum_a, sum_b])
            if k:
                leaving.append(joined.astype(jnp.float16))
            else:
                total = joined
            if k:
                parts.append(move(leaving[-1], pairs_around(count, depth - k)))
        sent = tuple(leaving)
    for value in parts:
        total = total + wide(value)
    grad = (1.0 / lift) * total

    first_new = beta_one * moment[0] + (1.0 - beta_one) * grad
    squares_new = beta_two * second[0] + (1.0 - beta_two) * grad * grad
    step = first_new / bias_one / (jnp.sqrt(squares_new / bias_two) + epsilon)
    current = matrix.astype(jnp.float32)
    updated = current - learn_rate * (step + decay_rate * current)
    delta = (updated - current).astype(jnp.bfloat16)

    groups = lax.axis_size("expert")
    mine = lax.axis_index("expert")
    wanted = pick(placement, mine)[:, None, None]
    incoming = jnp.where(wanted == mine, delta[None], jnp.zeros_like(delta)[None])
    for shift in range(1, groups):
        ring = [(e, (e + shift) % groups) for e in range(groups)]
        other = move(delta, ring, "expert")
        source = lax.rem(mine + groups - shift, groups)
        incoming = jnp.where(wanted == source, other[None], incoming)
    served = serving[0].astype(jnp.float32) + incoming.astype(jnp.float32)

    if by_kernel:
        d_hid = None
        for some in (gathered[:-1], gathered[-1:]):
            d_hid = hidden_columns(place, limit, some, grads_out, d_hid, depth)
    else:
        blocks = {}
        for group, arrays in gathered:
            far_a, far_b = arrays[len(group) :]
            for m, k in enumerate(group):
                full_a = jnp.stack([arrays[m][0], far_a[m]], axis=1)
                full_b = jnp.stack([arrays[m][1], far_b[m]], axis=0)
                blocks[k] = jnp.stack([full_a, full_b], axis=2)
        full = jnp.stack([blocks[k] for k in range(depth)] * 2)
        full = lax.dynamic_slice_in_dim(full, depth - outer, depth, 0)
        full = jnp.where(upper == 0, full, jnp.flip(full, 1))
        full = jnp.where(lower == 0, full, jnp.flip(full, 2)).reshape(rows, width)
        live = jnp.arange(tokens, dtype=jnp.int32) < limit[0]
        d_full = scale * jnp.dot(grads_out, full.T, preferred_element_type=jnp.float32)
        d_hid = jnp.where(live[:, None], d_full, 0.0).astype(jnp.bfloat16)
    return (
        d_hid[None],
        updated.astype(jnp.bfloat16)[None],
        first_new[None],
        squares_new[None],
        served.astype(jnp.bfloat16)[None],
    )


def solution(mesh):
    placed = (
        P("expert", "dp", None),
        P("expert", "dp", None),
        P("expert", "dp"),
        P(),
        P("expert", "dp", None),
        P("expert", "dp", None),
        P("expert", "dp", None),
        P("expert", None, "dp", None),
    )
    return jax.shard_map(
        body,
        mesh=mesh,
        in_specs=placed,
        out_specs=(
            P("expert", "dp", None),
            P("expert", "dp", None),
            P("expert", "dp", None),
            P("expert", "dp", None),
            P("expert", None, "dp", None),
        ),
        check_vma=False,
    )
```

```python
import functools
import math

import jax
import jax.numpy as jnp
from jax import lax
from jax.experimental import pallas as pl
from jax.experimental.pallas import tpu as pltpu
from jax.sharding import PartitionSpec as P


beta_one = 0.9
beta_two = 0.95
bias_one = 1.0 - 0.9**20
bias_two = 1.0 - 0.95**20
learn_rate = 0.05
decay_rate = 0.1
epsilon = 1e-08
largest_input = 6.0
half_range = 60000.0


def pairs_across(count, bit):
    return [(i, i ^ bit) for i in range(count)]


def pairs_around(count, k):
    return [((i + 4 * k) % count, i) for i in range(count)]


def pairs_along(count, step, first, last):
    return [(i, i + step * 4) for i in range(count) if first <= i // 4 < last]


def move(value, pairs, axis="dp"):
    return lax.ppermute(value, axis, pairs)


def after(value, *earlier):
    return lax.optimization_barrier((value,) + earlier)[0] if earlier else value


def pick(stacked, at, axis=0):
    return lax.dynamic_index_in_dim(stacked, at, axis, keepdims=False)


def gather_groups(depth):
    return [[k] for k in sorted(range(depth), key=lambda k: max(k, depth - k) if k else 0)]


def reduce_groups(depth):
    offsets = list(range(1, depth)) + [0]
    return [offsets[: depth // 2], offsets[depth // 2 :]]


def rows_kernel(order, place, limit, acts, send, keep, turned):
    depth = 2 * len(order[0])
    half = turned.shape[0] // (8 * depth)
    outer, upper, lower = place[0] // 4, lax.rem(place[0] // 2, 2), lax.rem(place[0], 2)
    values = acts[...]
    at = lax.broadcasted_iota(jnp.int32, values.shape, 0)
    turned[...] = jnp.where(at < limit[0], values, jnp.zeros_like(values)).T
    for out, flipped in ((send, 1), (keep, 0)):
        target = 0
        for g, h in ((0, 0), (0, 1), (1, 0), (1, 1)):
            for k in order[g]:
                z = lax.rem(outer + k, depth)
                for j in range(2):
                    y = upper ^ (1 - j) if h == 0 else upper ^ flipped
                    x = lower ^ flipped if h == 0 else lower ^ (1 - j)
                    source = (((z * 2 + y) * 2 + x) * 2 + h) * half
                    out[pl.ds(target, half)] = turned[pl.ds(pl.multiple_of(source, half), half)]
                    target += half


def rows_by_owner(order, place, limit, acts):
    tokens, rows = acts.shape
    shape = jax.ShapeDtypeStruct((rows // 2, tokens), acts.dtype)
    return pl.pallas_call(
        functools.partial(rows_kernel, order),
        out_shape=(shape, shape),
        grid_spec=pltpu.PrefetchScalarGridSpec(
            num_scalar_prefetch=2,
            grid=(1,),
            in_specs=[pl.BlockSpec((tokens, rows), lambda i, *_: (0, 0))],
            out_specs=[pl.BlockSpec((rows // 2, tokens), lambda i, *_: (0, 0))] * 2,
            scratch_shapes=[pltpu.VMEM((rows, tokens), acts.dtype)],
        ),
        compiler_params=pltpu.CompilerParams(vmem_limit_bytes=20 * 2**20),
        name="rows_by_owner",
    )(place, limit, acts)


def hidden_kernel(offsets, depth, place, limit, *refs):
    columns, out, full, ready, done = refs[-5:]
    groups = [len(group) for group in offsets]
    upper, lower = lax.rem(place[0] // 2, 2), lax.rem(place[0], 2)
    half = full.shape[0] // (8 * sum(groups))

    def at(first, y, x, h):
        return pl.ds(pl.multiple_of(first + ((y * 2 + x) * 2 + h) * half, half), half)

    @pl.when(pl.program_id(0) == 0)
    def _():
        start, rest = 0, refs
        for size in groups:
            far_a, far_b = rest[size : size + 2]
            for m in range(size):
                first = (start + m) * 8 * half
                for j in range(2):
                    y, x = upper ^ j, lower ^ j
                    full[at(first, y, lower, 0)] = rest[m][0, j]
                    full[at(first, y, 1 - lower, 0)] = far_a[m, j]
                    full[at(first, upper, x, 1)] = rest[m][1, j]
                    full[at(first, 1 - upper, x, 1)] = far_b[m, j]
            start += size
            rest = rest[size + 2 :]

    product = lax.dot_general(
        columns[...], full[...], (((1,), (1,)), ((), ())), preferred_element_type=jnp.float32
    )
    product = columns.shape[1] ** (-0.5) * product
    height = product.shape[0]
    step = pl.program_id(0)
    token = step * height + lax.broadcasted_iota(jnp.int32, product.shape, 0)
    ready[step] = jnp.where(token < limit[0], product, 0.0).astype(ready.dtype)

    def copies(t):
        found = []
        for n, k in enumerate(k for group in offsets for k in group):
            slot = lax.rem(place[0] // 4 + k, depth)
            found.append(
                pltpu.make_async_copy(
                    ready.at[t, :, pl.ds(n * 8 * half, 8 * half)],
                    out.at[
                        pl.ds(pl.multiple_of(t * height, height), height),
                        pl.ds(pl.multiple_of(slot * 8 * half, 8 * half), 8 * half),
                    ],
                    done.at[t, n],
                )
            )
        return found

    for copy in copies(step):
        copy.start()

    @pl.when(step == pl.num_programs(0) - 1)
    def _():
        for t in range(ready.shape[0]):
            for copy in copies(t):
                copy.wait()


def hidden_columns(place, limit, groups, columns, so_far, depth):
    tokens, width = columns.shape
    offsets = [group for group, _ in groups]
    blocks = sum(len(group) for group in offsets)
    block = 8 * groups[0][1][0].shape[2]
    steps = 2

    def same(array):
        zeros = (0,) * array.ndim
        return pl.BlockSpec(array.shape, lambda t, *_: zeros, pipeline_mode=pl.Buffered(1))

    args = [place, limit] + [array for _, arrays in groups for array in arrays] + [columns]
    in_specs = [same(array) for array in args[2:-1]]
    in_specs.append(pl.BlockSpec((tokens // steps, width), lambda t, *_: (t, 0)))
    kernel, aliases = functools.partial(hidden_kernel, offsets, depth), {}
    if so_far is not None:
        in_specs.insert(0, pl.BlockSpec(memory_space=pl.ANY))
        args.insert(2, so_far)
        aliases = {2: 0}
        inner = kernel
        kernel = lambda place, limit, so_far, *refs: inner(place, limit, *refs)
    return pl.pallas_call(
        kernel,
        out_shape=jax.ShapeDtypeStruct((tokens, depth * block), jnp.bfloat16),
        grid_spec=pltpu.PrefetchScalarGridSpec(
            num_scalar_prefetch=2,
            grid=(steps,),
            in_specs=in_specs,
            out_specs=pl.BlockSpec(memory_space=pl.ANY),
            scratch_shapes=[
                pltpu.VMEM((blocks * block, width), jnp.bfloat16),
                pltpu.VMEM((steps, tokens // steps, blocks * block), jnp.bfloat16),
                pltpu.SemaphoreType.DMA((steps, blocks)),
            ],
        ),
        input_output_aliases=aliases,
        cost_estimate=pl.CostEstimate(
            flops=2 * tokens * width * block * blocks,
            transcendentals=0,
            bytes_accessed=2 * tokens * width,
        ),
        compiler_params=pltpu.CompilerParams(vmem_limit_bytes=24 * 2**20),
        name="hidden_columns",
    )(*args)


def body(hidden, cotangent, counts, placement, weight, moment, second, serving):
    acts = hidden[0]
    grads_out = cotangent[0]
    matrix = weight[0]
    tokens, rows = acts.shape
    owned, width = matrix.shape
    scale = width ** (-0.5)
    count = lax.axis_size("dp")
    depth = count // 4
    index = lax.axis_index("dp")
    outer, upper, lower = index // 4, lax.rem(index // 2, 2), lax.rem(index, 2)
    half = owned // 2
    place = jnp.full((1,), index, jnp.int32)
    limit = counts[0]
    across_x, across_y = pairs_across(count, 1), pairs_across(count, 2)
    by_kernel = half % 16 == 0

    bound = count * tokens * largest_input**2 * scale
    lift = 2.0 ** math.floor(math.log2(half_range / bound))

    own_a, own_b = matrix[:half], matrix[half:]
    other_a = move(own_a, across_y)
    other_b = move(own_b, across_x)
    base = jnp.stack([jnp.stack([own_a, other_a]), jnp.stack([own_b, other_b])])
    below, above = {}, {}
    up = down = base
    for t in range(1, depth):
        up = below[t] = move(up, pairs_along(count, 1, t - 1, depth - 1))
        down = above[t] = move(down, pairs_along(count, -1, 1, depth - t + 1))
    near = {0: base}
    for g, group in enumerate(gather_groups(depth)[1:], 1):
        for k in group:
            near[k] = jnp.where(outer + k < depth, above[k], below[depth - k])
    gathered = []
    for group in gather_groups(depth):
        far_a = move(jnp.stack([near[k][0] for k in group]), across_x)
        far_b = move(jnp.stack([near[k][1] for k in group]), across_y)
        gathered.append((group, [near[k] for k in group] + [far_a, far_b]))

    order = reduce_groups(depth)
    if by_kernel:
        send_rows, keep_rows = rows_by_owner(order, place, limit, acts)
    else:
        live = jnp.arange(tokens, dtype=jnp.int32) < limit[0]
        turned = jnp.where(live[:, None], acts, jnp.zeros_like(acts)).T
        turned = turned.reshape(depth, 2, 2, 2, half, tokens)
        turned = jnp.stack([pick(turned, lax.rem(outer + k, depth)) for k in sum(order, [])])

        def by_side(flipped):
            part_a = pick(turned[:, :, :, 0], lower ^ flipped, 2)
            part_b = pick(turned[:, :, :, 1], upper ^ flipped, 1)
            part_a = jnp.stack([pick(part_a, 1 - upper, 1), pick(part_a, upper, 1)], axis=1)
            part_b = jnp.stack([pick(part_b, 1 - lower, 1), pick(part_b, lower, 1)], axis=1)
            both = jnp.stack([part_a, part_b]).reshape(2, 2, depth // 2, 2, half, tokens)
            return jnp.swapaxes(both, 0, 1).reshape(-1, tokens)

        send_rows, keep_rows = by_side(1), by_side(0)

    def term(picked, kind):
        product = jnp.dot(picked, grads_out, preferred_element_type=jnp.float32)
        product = ((scale * lift) * product).astype(kind)
        return product.reshape(-1, 2, depth // 2, 2, half, width)

    def wide(value):
        return value.astype(jnp.float32)

    came = []
    for g in range(2):
        some = send_rows[g * rows // 4 : (g + 1) * rows // 4]
        send = term(some, jnp.float16)[0]
        came_a = move(send[0], across_x)
        came_b = move(send[1], across_y)
        came.append((came_a, came_b))
    keep = term(keep_rows, jnp.float32)
    sent, middle = (), []
    for g in range(2):
        came_a, came_b = came[g]
        kept = after(keep, *sent)
        out_a = (kept[g, 0, :, 0] + wide(came_a[:, 0])).astype(jnp.float16)
        out_b = (kept[g, 1, :, 0] + wide(came_b[:, 0])).astype(jnp.float16)
        second_a = move(out_a, across_y)
        second_b = move(out_b, across_x)
        middle.append((second_a, second_b))
        sent = (out_a, out_b)
    parts, total = [], None
    for g in range(2):
        came_a, came_b = came[g]
        second_a, second_b = (after(value, *sent) for value in middle[g])
        leaving = []
        for n, k in enumerate(order[g]):
            sum_a = keep[g, 0, n, 1] + wide(came_a[n, 1]) + wide(second_a[n])
            sum_b = keep[g, 1, n, 1] + wide(came_b[n, 1]) + wide(second_b[n])
            joined = jnp.concatenate([sum_a, sum_b])
            if k:
                leaving.append(joined.astype(jnp.float16))
            else:
                total = joined
            if k:
                parts.append(move(leaving[-1], pairs_around(count, depth - k)))
        sent = tuple(leaving)
    for value in parts:
        total = total + wide(value)
    grad = (1.0 / lift) * total

    first_new = beta_one * moment[0] + (1.0 - beta_one) * grad
    squares_new = beta_two * second[0] + (1.0 - beta_two) * grad * grad
    step = first_new / bias_one / (jnp.sqrt(squares_new / bias_two) + epsilon)
    current = matrix.astype(jnp.float32)
    updated = current - learn_rate * (step + decay_rate * current)
    delta = (updated - current).astype(jnp.bfloat16)

    groups = lax.axis_size("expert")
    mine = lax.axis_index("expert")
    wanted = pick(placement, mine)[:, None, None]
    incoming = jnp.where(wanted == mine, delta[None], jnp.zeros_like(delta)[None])
    for shift in range(1, groups):
        ring = [(e, (e + shift) % groups) for e in range(groups)]
        other = move(delta, ring, "expert")
        source = lax.rem(mine + groups - shift, groups)
        incoming = jnp.where(wanted == source, other[None], incoming)
    served = serving[0].astype(jnp.float32) + incoming.astype(jnp.float32)
    served = served.astype(jnp.bfloat16)

    if by_kernel:
        d_hid = None
        for some in gathered:
            d_hid = hidden_columns(place, limit, [some], grads_out, d_hid, depth)
    else:
        blocks = {}
        for group, arrays in gathered:
            far_a, far_b = arrays[len(group) :]
            for m, k in enumerate(group):
                full_a = jnp.stack([arrays[m][0], far_a[m]], axis=1)
                full_b = jnp.stack([arrays[m][1], far_b[m]], axis=0)
                blocks[k] = jnp.stack([full_a, full_b], axis=2)
        full = jnp.stack([blocks[k] for k in range(depth)] * 2)
        full = lax.dynamic_slice_in_dim(full, depth - outer, depth, 0)
        full = jnp.where(upper == 0, full, jnp.flip(full, 1))
        full = jnp.where(lower == 0, full, jnp.flip(full, 2)).reshape(rows, width)
        live = jnp.arange(tokens, dtype=jnp.int32) < limit[0]
        d_full = scale * jnp.dot(grads_out, full.T, preferred_element_type=jnp.float32)
        d_hid = jnp.where(live[:, None], d_full, 0.0).astype(jnp.bfloat16)
    return (
        d_hid[None],
        updated.astype(jnp.bfloat16)[None],
        first_new[None],
        squares_new[None],
        served[None],
    )


def solution(mesh):
    placed = (
        P("expert", "dp", None),
        P("expert", "dp", None),
        P("expert", "dp"),
        P(),
        P("expert", "dp", None),
        P("expert", "dp", None),
        P("expert", "dp", None),
        P("expert", None, "dp", None),
    )
    return jax.shard_map(
        body,
        mesh=mesh,
        in_specs=placed,
        out_specs=(
            P("expert", "dp", None),
            P("expert", "dp", None),
            P("expert", "dp", None),
            P("expert", "dp", None),
            P("expert", None, "dp", None),
        ),
        check_vma=False,
    )
```
